512 devices in a mesh: row: 32 (over z, x), col: 16 (over y, core).
Axes of the slice: x: 4, y: 8, z: 8, core: 2. Of those that a mesh axis runs over, the one named last changes fastest.
Arguments:
- trailing: bfloat16 [65536, 8192], P('row', 'col'), may hold values from -6 to 6
- panel: float32 [65536, 256], P(('row', 'col')), may hold values from -1 to 1
- diag_inverse: float32 [256, 256], P(None, 'col'), may hold values from -1 to 2, as said below
Outputs:
- updated: bfloat16 [65536, 8192], P('row', 'col')
The draws below stay inside these ranges and needn't reach their ends.
Inputs may be any that keep to these rules, and one draw needn't show every extreme that they name: `diag_inverse`: lower triangular with a positive diagonal.
All inputs are finite; a program needn't handle non-finite values.
Results may differ from the reference program's by a relative error of at most 0.0051.
Values may be sent and summed in bfloat16 or wider, within the bound.
A program may use at most 64 MiB of HBM per device.

```python
import math
import jax
import jax.numpy as jnp
from jax import lax

NB = 256
SBLK = 2
ROWS_DEV = 2048
ORDER = 65536
SLAB = 8192
N_ROW = 32
N_COL = 16


def draw_diag_inverse(key, part):
    key_off, key_diag = jax.random.split(key)
    row_ids = lax.broadcasted_iota(jnp.int32, (NB, NB), 0)
    col_ids = lax.broadcasted_iota(jnp.int32, (NB, NB), 1)
    lower_part = jnp.clip(jax.random.normal(key_off, (NB, NB), jnp.float32), -4.0, 4.0) / math.sqrt(NB)
    diagonal = jax.random.uniform(key_diag, (NB, NB), jnp.float32, 1.0, 2.0)
    return jnp.where(row_ids == col_ids, diagonal, jnp.where(row_ids > col_ids, lower_part, 0.0))


def block_levels(stream_key, extent, shards, low, high):
    def one(dim, shards_of):
        steps = jax.random.uniform(jax.random.fold_in(jax.random.fold_in(stream_key, 6), dim), (shards_of,), jnp.float32, low / len(shards), high / len(shards))
        return jnp.repeat(jnp.exp(steps), extent[dim] // shards_of).reshape((-1,) + (1,) * (len(extent) - dim - 1))

    gain = one(*shards[0])
    for cut in shards[1:]:
        gain = gain * one(*cut)
    return gain


def scatter_about(own_key, shape, scale, most, cuts=(), dtype=jnp.bfloat16):
    values = jax.random.normal(own_key, shape, jnp.float32) * scale
    if len(cuts) > 0:
        values = block_levels(own_key, shape, cuts, -0.22, 0.18) * values
    return jnp.clip(values, min=-most, max=most).astype(dtype)


def setup_inputs(seed: int = 0) -> dict:
    key_list = jax.random.split(jax.random.key(seed), 4)
    trailing = scatter_about(key_list[0], (ORDER, SLAB), 1.0, 6.0, ((0, 32), (1, 16)))
    panel = scatter_about(key_list[1], (ORDER, NB), 0.17, 1.0, ((0, 512),), jnp.float32)
    diag_inverse = draw_diag_inverse(jax.random.fold_in(key_list[3], 71), 0)
    return {"trailing": trailing, "panel": panel, "diag_inverse": diag_inverse}


def reference(trailing, panel, diag_inverse):
    solved = jnp.dot(panel, diag_inverse.T, precision=lax.Precision.HIGHEST, preferred_element_type=jnp.float32).astype(jnp.bfloat16)
    grouped = solved.reshape(N_ROW, ROWS_DEV, NB)
    tops = grouped[:SBLK * N_COL, :NB, :]
    mirror = tops.reshape(SBLK, N_COL, NB, NB).transpose(1, 0, 2, 3).reshape(SLAB, NB)
    slabs = trailing.reshape(N_ROW, ROWS_DEV, SLAB)

    def one_block(pair):
        slab_rows, solved_rows = pair
        product = jnp.dot(solved_rows, mirror.T, preferred_element_type=jnp.float32)
        return (slab_rows.astype(jnp.float32) - product).astype(jnp.bfloat16)

    result = lax.map(one_block, (slabs, grouped))
    return result.reshape(ORDER, SLAB)
```

```python
import jax
import jax.numpy as jnp
from jax import lax
from jax.experimental import pallas as pl
from jax.experimental.pallas import tpu as pltpu
from jax.sharding import PartitionSpec as P

MESH = pl.DeviceIdType.MESH
NB = 256
NX, NZ, NY = 4, 8, 8
N_COL = 16
OWN = 128
PIECE = 16
HIGHEST = lax.Precision.HIGHEST


def remote(src, dst, send_sem, recv_sem, device):
    return pltpu.make_async_remote_copy(
        src_ref=src, dst_ref=dst, send_sem=send_sem, recv_sem=recv_sem,
        device_id=device, device_id_type=MESH,
    )


def take(ref, sem):
    pltpu.make_async_copy(ref, ref, sem).wait()


def far_first(n, size):
    half = size // 2
    return half + (1 - 2 * lax.rem(n, 2)) * lax.div(n + 1, 2)


def step_kernel(
    trailing, panel, dinv, out,
    slab, rows, dcol, dt, raw, sol, mir,
    load_sem, d_send, d_recv, dsib_send, dsib_recv, raw_send, raw_recv,
    ring_send, ring_recv, half_recv, sib_send, sib_recv, mir_send, mir_recv, out_sem,
):
    r, c = lax.axis_index("row"), lax.axis_index("col")
    x, z = lax.rem(r, NX), lax.div(r, NX)
    y, k = lax.div(c, 2), lax.rem(c, 2)
    sibling = (r, 2 * y + 1 - k)

    def at_y(step):
        return (r, lax.rem(y + step, NY) * 2 + k)

    def plane(n):
        dz = far_first(lax.div(n, NX), NZ)
        dx = far_first(lax.rem(n, NX), NX)
        return (lax.rem(z + dz, NZ) * NX + lax.rem(x + dx, NX), c)

    load_panel = pltpu.make_async_copy(panel, rows, load_sem.at[0])
    load_dinv = pltpu.make_async_copy(dinv, dcol, load_sem.at[1])
    load_slab = pltpu.make_async_copy(trailing, slab, load_sem.at[2])
    load_dinv.start()
    load_panel.start()
    load_slab.start()

    origin = (c + N_COL * lax.div(r, N_COL), lax.div(lax.rem(r, N_COL), 8))
    from_self = jnp.logical_and(origin[0] == r, origin[1] == c)
    sends_raw = c < 2

    barrier = pltpu.get_barrier_semaphore()

    def hello_plane(n, carry):
        pl.semaphore_signal(barrier, inc=1, device_id=plane(n), device_id_type=MESH)
        return carry

    @pl.when(jnp.logical_not(from_self))
    def _():
        pl.semaphore_signal(barrier, inc=1, device_id=origin, device_id_type=MESH)

    lax.fori_loop(0, 31, hello_plane, 0)
    for step in range(1, NY):
        pl.semaphore_signal(barrier, inc=1, device_id=at_y(step), device_id_type=MESH)
    pl.semaphore_signal(barrier, inc=1, device_id=sibling, device_id_type=MESH)

    load_dinv.wait()
    def d_rows(yy, kk):
        return dt.at[pl.ds(pl.multiple_of(lax.rem(yy, NY) * 32 + kk * 16, 16), 16), :]

    d_rows(y, k)[...] = dcol[...]
    load_panel.wait()

    self_piece = jnp.where(from_self, 1, 0)
    pl.semaphore_wait(barrier, 39 + jnp.where(sends_raw, 8 - self_piece, 0))

    far_order = (4, 3, 5, 2, 6, 1, 7)
    d_copies = [remote(d_rows(y, k), d_rows(y, k), d_send.at[i], d_recv.at[i], at_y(i)) for i in far_order]
    for copy in d_copies:
        copy.start()
    d_own = remote(d_rows(y, k), d_rows(y, k), dsib_send.at[0], dsib_recv.at[0], sibling)
    d_own.start()

    def raw_target(i):
        return (N_COL * lax.div(r, N_COL) + 8 * k + i, lax.rem(r, N_COL))

    def raw_rows(i):
        return rows.at[pl.ds(i * PIECE, PIECE), :]

    def raw_is_self(i):
        target = raw_target(i)
        return jnp.logical_and(target[0] == r, target[1] == c)

    @pl.when(sends_raw)
    def _():
        for i in range(8):
            @pl.when(raw_is_self(i))
            def _():
                pltpu.make_async_copy(raw_rows(i), raw, raw_recv).start()

            @pl.when(jnp.logical_not(raw_is_self(i)))
            def _():
                remote(raw_rows(i), raw, raw_send.at[i], raw_recv, raw_target(i)).start()

    d_handed = []
    for i in (1, 7, 2, 6, 3, 5, 4):
        ref = d_rows(y + NY - i, k)
        take(ref, d_recv.at[i])
        copy = remote(ref, ref, dsib_send.at[i], dsib_recv.at[i], sibling)
        copy.start()
        d_handed.append(copy)
    for i in range(NY):
        take(d_rows(y + NY - i, 1 - k), dsib_recv.at[i])

    def solve(values):
        return lax.dot_general(
            values, dt[...], (((1,), (0,)), ((), ())), precision=HIGHEST, preferred_element_type=jnp.float32
        ).astype(jnp.bfloat16)

    def shard(yy, kk):
        return sol.at[pl.ds(pl.multiple_of(lax.rem(yy, NY) * 256 + kk * OWN, OWN), OWN), :]

    def half(yy, kk, j):
        return sol.at[pl.ds(pl.multiple_of(lax.rem(yy, NY) * 256 + kk * OWN + j * 64, 64), 64), :]

    mine = shard(y, k)
    mine[...] = solve(rows[...])
    sends = []

    def go(src, send_sem, recv_sem, device):
        copy = remote(src, src, send_sem, recv_sem, device)
        copy.start()
        sends.append(copy)

    go(mine, ring_send.at[2], ring_recv.at[2], at_y(2))
    go(mine, ring_send.at[6], ring_recv.at[6], at_y(6))
    go(mine, ring_send.at[1], ring_recv.at[1], at_y(1))
    go(mine, ring_send.at[7], ring_recv.at[7], at_y(7))
    go(mine, sib_send.at[0], sib_recv.at[0], sibling)

    take(raw, raw_recv)
    mir[r] = solve(raw[...])

    def spread(n, carry):
        remote(mir.at[r], mir.at[r], mir_send, mir_recv, plane(n)).start()
        return carry

    lax.fori_loop(0, 31, spread, 0)

    take(shard(y + 6, k), ring_recv.at[2])
    go(half(y + 6, k, 0), ring_send.at[4], half_recv.at[0], at_y(2))
    go(shard(y + 6, k), ring_send.at[3], ring_recv.at[3], at_y(1))
    go(shard(y + 6, k), sib_send.at[2], sib_recv.at[2], sibling)
    take(shard(y + 2, k), ring_recv.at[6])
    go(half(y + 2, k, 1), ring_send.at[8], half_recv.at[1], at_y(6))
    go(shard(y + 2, k), ring_send.at[5], ring_recv.at[5], at_y(7))
    go(shard(y + 2, k), sib_send.at[6], sib_recv.at[6], sibling)
    for i in (1, 7, 3, 5):
        take(shard(y + NY - i, k), ring_recv.at[i])
        go(shard(y + NY - i, k), sib_send.at[i], sib_recv.at[i], sibling)
    take(half(y + 4, k, 0), half_recv.at[0])
    take(half(y + 4, k, 1), half_recv.at[1])
    go(shard(y + 4, k), sib_send.at[4], sib_recv.at[4], sibling)

    load_slab.wait()
    take(mir.at[pl.ds(0, 31)], mir_recv)
    mirror = mir[...].reshape(2 * NB, NB)
    stores = []
    for n, i in enumerate((0, 2, 6, 1, 7, 3, 5, 4)):
        take(shard(y + NY - i, 1 - k), sib_recv.at[i])
        span = pl.ds(pl.multiple_of(lax.rem(y + NY - i, NY) * 256, 256), 256)
        product = lax.dot_general(
            sol[span, :], mirror, (((1,), (1,)), ((), ())), preferred_element_type=jnp.float32
        )
        slab[span, :] = (slab[span, :].astype(jnp.float32) - product).astype(jnp.bfloat16)
        store = pltpu.make_async_copy(slab.at[span, :], out.at[span, :], out_sem.at[n])
        store.start()
        stores.append(store)

    for copy in d_copies + d_handed + [d_own] + sends:
        copy.wait_send()
    take(mir.at[pl.ds(0, 31)], mir_send)

    @pl.when(sends_raw)
    def _():
        for i in range(8):
            @pl.when(jnp.logical_not(raw_is_self(i)))
            def _():
                remote(raw_rows(i), raw, raw_send.at[i], raw_recv, raw_target(i)).wait_send()

    for store in stores:
        store.wait()


def local(trailing, panel, diag_inverse):
    dma = pltpu.SemaphoreType.DMA
    any_space = pl.BlockSpec(memory_space=pl.ANY)
    hbm = pl.BlockSpec(memory_space=pltpu.HBM)
    return pl.pallas_call(
        step_kernel,
        out_shape=jax.ShapeDtypeStruct(trailing.shape, trailing.dtype),
        in_specs=[hbm] * 3,
        out_specs=any_space,
        scratch_shapes=[
            pltpu.VMEM((2048, 512), jnp.bfloat16),
            pltpu.VMEM((128, 256), jnp.float32),
            pltpu.VMEM((16, 256), jnp.float32),
            pltpu.VMEM((256, 256), jnp.float32),
            pltpu.VMEM((16, 256), jnp.float32),
            pltpu.VMEM((2048, 256), jnp.bfloat16),
            pltpu.VMEM((32, 16, 256), jnp.bfloat16),
            dma((3,)), dma((8,)), dma((8,)), dma((8,)), dma((8,)), dma((8,)), dma(()),
            dma((9,)), dma((8,)), dma((2,)), dma((8,)), dma((8,)), dma(()), dma(()), dma((8,)),
        ],
        name="panel_step",
        compiler_params=pltpu.CompilerParams(
            collective_id=0, has_side_effects=True, vmem_limit_bytes=60 * 1024 * 1024
        ),
    )(trailing, panel, diag_inverse.T)


def solution(mesh):
    in_specs = (P("row", "col"), P(("row", "col"), None), P(None, "col"))
    out_specs = P("row", "col")
    return jax.shard_map(local, mesh=mesh, in_specs=in_specs, out_specs=out_specs, check_vma=False)
```

```python
import jax
import jax.numpy as jnp
from jax import lax
from jax.experimental import pallas as pl
from jax.experimental.pallas import tpu as pltpu
from jax.sharding import PartitionSpec as P

MESH = pl.DeviceIdType.MESH
NB = 256
NY = 8
N_COL = 16
OWN = 128
PIECE = 16
HIGHEST = lax.Precision.HIGHEST


def remote(src, dst, send_sem, recv_sem, device):
    return pltpu.make_async_remote_copy(
        src_ref=src, dst_ref=dst, send_sem=send_sem, recv_sem=recv_sem,
        device_id=device, device_id_type=MESH,
    )


def take(ref, sem):
    pltpu.make_async_copy(ref, ref, sem).wait()


HALF_PEERS = (10, 14, 8, 9, 11, 12, 13, 15, 6, 2, 4, 5, 7, 1, 3)


def step_kernel(
    trailing, panel, dinv, out,
    slab, rows, dt, raw, sol, mir,
    load_sem, d_send, d_recv, dsib_send, dsib_recv, raw_send, pass_send, raw_recv,
    ready, ring_send, ring_recv, half_recv, sib_send, sib_recv, mir_send, mir_recv, out_sem,
):
    r, c = lax.axis_index("row"), lax.axis_index("col")
    y, k = c >> 1, c & 1
    sibling = (r, c ^ 1)
    block = r >> 4
    slot = r & 15
    early = block == 0
    late = block == 1
    is_origin = c < 2
    own_origin = jnp.logical_and(r == 0, c == 0)

    def at_y(step):
        return (r, (c + 2 * step) & 15)

    def d_rows(yy, kk):
        return dt.at[pl.ds(pl.multiple_of((yy & 7) * 32 + kk * 16, 16), 16), :]

    load_panel = pltpu.make_async_copy(panel, rows, load_sem.at[0])
    load_dinv = pltpu.make_async_copy(dinv, d_rows(y, k), load_sem.at[1])
    load_slab = pltpu.make_async_copy(trailing, slab, load_sem.at[2])
    load_panel.start()
    load_dinv.start()
    load_slab.start()

    barrier = pltpu.get_barrier_semaphore()

    def greet(device):
        pl.semaphore_signal(barrier, inc=1, device_id=device, device_id_type=MESH)

    @pl.when(early)
    def _():
        greet((c + N_COL, r >> 3))
        greet((r + N_COL, c))

        @pl.when(jnp.logical_not(own_origin))
        def _():
            greet((c, r >> 3))

    for n in range(1, N_COL):
        greet((r, c ^ n))
    for n in HALF_PEERS:
        greet((r ^ n, c))

    def shard(yy, kk):
        return sol.at[pl.ds(pl.multiple_of((yy & 7) * 256 + kk * OWN, OWN), OWN), :]

    def half(yy, kk, j):
        return sol.at[pl.ds(pl.multiple_of((yy & 7) * 256 + kk * OWN + j * 64, 64), 64), :]

    mine = shard(y, k)
    load_panel.wait()
    mine[...] = rows[...].astype(jnp.bfloat16)
    load_dinv.wait()
    pl.semaphore_wait(
        barrier, 30 + block + jnp.where(is_origin, 8, 0) - jnp.where(own_origin, 1, 0)
    )

    def direct(i):
        src = rows.at[pl.ds(i * PIECE, PIECE), :]
        return remote(src, raw.at[block], raw_send.at[i], raw_recv.at[block], (8 * k + i, slot))

    @pl.when(is_origin)
    def _():
        @pl.when(jnp.logical_not(own_origin))
        def _():
            direct(0).start()

        @pl.when(own_origin)
        def _():
            pltpu.make_async_copy(rows.at[pl.ds(0, PIECE), :], raw.at[0], raw_recv.at[0]).start()

        for i in range(1, 8):
            direct(i).start()

    d_copies = [
        remote(d_rows(y, k), d_rows(y, k), d_send.at[i], d_recv.at[i], at_y(i)) for i in (4, 3, 5, 2, 6, 1, 7)
    ]
    for copy in d_copies:
        copy.start()
    d_own = remote(d_rows(y, k), d_rows(y, k), dsib_send.at[0], dsib_recv.at[0], sibling)
    d_own.start()

    @pl.when(late)
    def _():
        pl.semaphore_signal(ready, inc=1, device_id=(r - N_COL, c), device_id_type=MESH)

    sends = []

    def go(src, send_sem, recv_sem, device):
        copy = remote(src, src, send_sem, recv_sem, device)
        copy.start()
        sends.append(copy)

    go(mine, ring_send.at[2], ring_recv.at[2], at_y(2))
    go(mine, ring_send.at[6], ring_recv.at[6], at_y(6))
    go(mine, ring_send.at[1], ring_recv.at[1], at_y(1))
    go(mine, ring_send.at[7], ring_recv.at[7], at_y(7))
    go(mine, sib_send.at[0], sib_recv.at[0], sibling)

    def hand_d(i):
        ref = d_rows(y - i, k)
        take(ref, d_recv.at[i])
        copy = remote(ref, ref, dsib_send.at[i], dsib_recv.at[i], sibling)
        copy.start()
        sends.append(copy)

    for i in (1, 7, 2, 6):
        hand_d(i)
    take(shard(y - 2, k), ring_recv.at[2])
    go(half(y - 2, k, 0), ring_send.at[4], half_recv.at[0], at_y(2))
    go(shard(y - 2, k), ring_send.at[3], ring_recv.at[3], at_y(1))
    go(shard(y - 2, k), sib_send.at[2], sib_recv.at[2], sibling)
    take(shard(y + 2, k), ring_recv.at[6])
    go(half(y + 2, k, 1), ring_send.at[8], half_recv.at[1], at_y(6))
    go(shard(y + 2, k), ring_send.at[5], ring_recv.at[5], at_y(7))
    go(shard(y + 2, k), sib_send.at[6], sib_recv.at[6], sibling)
    for i in (3, 5, 4):
        hand_d(i)
    for i in (1, 7):
        take(shard(y - i, k), ring_recv.at[i])
        go(shard(y - i, k), sib_send.at[i], sib_recv.at[i], sibling)
    for i in range(NY):
        take(d_rows(y - i, 1 - k), dsib_recv.at[i])

    def hand_raw(b):
        return remote(raw.at[b], raw.at[b], pass_send.at[b], raw_recv.at[b], (r + N_COL, c))

    def spread(b):
        take(raw.at[b], raw_recv.at[b])

        @pl.when(early)
        def _():
            if b == 0:
                pl.semaphore_wait(ready, 1)
            hand_raw(b).start()

        solved = lax.dot_general(
            raw[b], dt[...], (((1,), (0,)), ((), ())), precision=HIGHEST, preferred_element_type=jnp.float32
        ).astype(jnp.bfloat16).astype(jnp.float32)
        piece = mir.at[b * 16 + slot]
        piece[...] = lax.dot_general(
            solved, dt[...], (((1,), (1,)), ((), ())), precision=HIGHEST, preferred_element_type=jnp.float32
        ).astype(jnp.bfloat16)
        for n in HALF_PEERS:
            remote(piece, piece, mir_send, mir_recv.at[b], (r ^ n, c)).start()

    spread(0)
    for i in (3, 5):
        take(shard(y - i, k), ring_recv.at[i])
        go(shard(y - i, k), sib_send.at[i], sib_recv.at[i], sibling)
    take(half(y + 4, k, 0), half_recv.at[0])
    take(half(y + 4, k, 1), half_recv.at[1])
    go(shard(y + 4, k), sib_send.at[4], sib_recv.at[4], sibling)
    spread(1)

    load_slab.wait()
    for i in (0, 2, 6, 1, 7, 3, 5, 4):
        take(shard(y - i, 1 - k), sib_recv.at[i])
    stores = []
    for b in range(2):
        take(mir.at[pl.ds(0, 15)], mir_recv.at[b])
        mirror = mir[b * 16:b * 16 + 16].reshape(NB, NB)
        cols = slice(b * NB, b * NB + NB)
        product = lax.dot_general(
            sol[...], mirror, (((1,), (1,)), ((), ())), preferred_element_type=jnp.float32
        )
        slab[:, cols] = (slab[:, cols].astype(jnp.float32) - product).astype(jnp.bfloat16)
        store = pltpu.make_async_copy(slab.at[:, cols], out.at[:, cols], out_sem.at[b])
        store.start()
        stores.append(store)

    for copy in d_copies + [d_own] + sends:
        copy.wait_send()
    take(mir.at[pl.ds(0, 30)], mir_send)

    @pl.when(is_origin)
    def _():
        @pl.when(jnp.logical_not(own_origin))
        def _():
            direct(0).wait_send()

        for i in range(1, 8):
            direct(i).wait_send()

    @pl.when(early)
    def _():
        for b in range(2):
            hand_raw(b).wait_send()

    for store in stores:
        store.wait()


def local(trailing, panel, diag_inverse):
    dma = pltpu.SemaphoreType.DMA
    any_space = pl.BlockSpec(memory_space=pl.ANY)
    hbm = pl.BlockSpec(memory_space=pltpu.HBM)
    trailing, panel, dinv = (
        pltpu.with_memory_space_constraint(v, pltpu.HBM) for v in (trailing, panel, diag_inverse.T)
    )
    return pl.pallas_call(
        step_kernel,
        out_shape=jax.ShapeDtypeStruct(trailing.shape, trailing.dtype),
        in_specs=[hbm] * 3,
        out_specs=any_space,
        scratch_shapes=[
            pltpu.VMEM((2048, 512), jnp.bfloat16),
            pltpu.VMEM((128, 256), jnp.float32),
            pltpu.VMEM((256, 256), jnp.float32),
            pltpu.VMEM((2, 16, 256), jnp.float32),
            pltpu.VMEM((2048, 256), jnp.bfloat16),
            pltpu.VMEM((32, 16, 256), jnp.bfloat16),
            dma((3,)), dma((8,)), dma((8,)), dma((8,)), dma((8,)), dma((8,)), dma((2,)), dma((2,)),
            pltpu.SemaphoreType.REGULAR(()),
            dma((9,)), dma((8,)), dma((2,)), dma((8,)), dma((8,)), dma(()), dma((2,)), dma((2,)),
        ],
        name="panel_step",
        compiler_params=pltpu.CompilerParams(
            collective_id=0, has_side_effects=True, vmem_limit_bytes=40 * 1024 * 1024
        ),
    )(trailing, panel, dinv)


def solution(mesh):
    in_specs = (P("row", "col"), P(("row", "col"), None), P(None, "col"))
    out_specs = P("row", "col")
    return jax.shard_map(local, mesh=mesh, in_specs=in_specs, out_specs=out_specs, check_vma=False)
```

```python
import jax
import jax.numpy as jnp
from jax import lax
from jax.experimental import pallas as pl
from jax.experimental.pallas import tpu as pltpu
from jax.sharding import PartitionSpec as P

MESH = pl.DeviceIdType.MESH
NB = 256
NY = 8
N_COL = 16
OWN = 128
PIECE = 16
HIGHEST = lax.Precision.HIGHEST


def remote(src, dst, send_sem, recv_sem, device):
    return pltpu.make_async_remote_copy(
        src_ref=src, dst_ref=dst, send_sem=send_sem, recv_sem=recv_sem,
        device_id=device, device_id_type=MESH,
    )


def take(ref, sem):
    pltpu.make_async_copy(ref, ref, sem).wait()


HALF_PEERS = (10, 14, 8, 9, 11, 12, 13, 15, 6, 2, 4, 5, 7, 1, 3)


def step_kernel(
    trailing, panel, dinv, out,
    slab, rows, dt, raw, sol, mir,
    load_sem, d_send, d_recv, dsib_send, dsib_recv, raw_send, pass_send, pass_recv, raw_recv,
    ready, origin_ready, two_send, two_recv, half_send, half_recv, three_send, three_recv, ring_send, ring_recv, sib_send, sib_recv,
    mir_send, mir_recv, out_sem,
):
    r, c = lax.axis_index("row"), lax.axis_index("col")
    y, k = c >> 1, c & 1
    sibling = (r, c ^ 1)
    block = r >> 4
    slot = r & 15
    early = block == 0
    late = block == 1
    is_origin = c < 2
    own_origin = jnp.logical_and(r == 0, c == 0)

    def at_y(step):
        return (r, (c + 2 * step) & 15)

    def d_rows(yy, kk):
        return dt.at[pl.ds(pl.multiple_of((yy & 7) * 32 + kk * 16, 16), 16), :]

    load_panel = pltpu.make_async_copy(panel, rows, load_sem.at[0])
    load_dinv = pltpu.make_async_copy(dinv, d_rows(y, k), load_sem.at[1])
    load_slab = pltpu.make_async_copy(trailing, slab, load_sem.at[2])
    load_panel.start()
    load_dinv.start()
    load_slab.start()

    barrier = pltpu.get_barrier_semaphore()

    def greet(device):
        pl.semaphore_signal(barrier, inc=1, device_id=device, device_id_type=MESH)

    @pl.when(early)
    def _():
        greet((c + N_COL, r >> 3))
        greet((r + N_COL, c))

        @pl.when(jnp.logical_not(own_origin))
        def _():
            greet((c, r >> 3))

    late_origin = jnp.logical_and(late, is_origin)
    late_other = jnp.logical_and(late, jnp.logical_not(is_origin))
    for n in range(1, N_COL):
        @pl.when(jnp.logical_not(jnp.logical_and(late_other, (c ^ n) < 2)))
        def _():
            greet((r, c ^ n))

    for n in HALF_PEERS:
        greet((r ^ n, c))

    def shard(yy, kk):
        return sol.at[pl.ds(pl.multiple_of((yy & 7) * 256 + kk * OWN, OWN), OWN), :]

    def half(yy, kk, j):
        return sol.at[pl.ds(pl.multiple_of((yy & 7) * 256 + kk * OWN + j * 64, 64), 64), :]

    mine = shard(y, k)
    load_panel.wait()
    mine[...] = rows[...].astype(jnp.bfloat16)
    load_dinv.wait()
    pl.semaphore_wait(barrier, 30 + block + jnp.where(is_origin, 8, 0) - jnp.where(own_origin, 1, 0) - jnp.where(late_origin, 14, 0))

    def direct(i):
        src = rows.at[pl.ds(i * PIECE, PIECE), :]
        return remote(src, raw.at[block], raw_send.at[i], raw_recv.at[block], (8 * k + i, slot))

    @pl.when(is_origin)
    def _():
        @pl.when(jnp.logical_not(own_origin))
        def _():
            direct(0).start()

        @pl.when(own_origin)
        def _():
            pltpu.make_async_copy(rows.at[pl.ds(0, PIECE), :], raw.at[0], raw_recv.at[0]).start()

        for i in range(1, 8):
            direct(i).start()

    @pl.when(late)
    def _():
        pl.semaphore_signal(ready, inc=1, device_id=(r - N_COL, c), device_id_type=MESH)

    def go(src, send_sem, recv_sem, device):
        copy = remote(src, src, send_sem, recv_sem, device)
        copy.start()

    def hand_d(i):
        ref = d_rows(y - i, k)
        take(ref, d_recv.at[i])
        copy = remote(ref, ref, dsib_send.at[i], dsib_recv.at[i], sibling)
        copy.start()

    def second_step(h):
        for way, (origin, one, two) in enumerate(((y - 2, 1, 2), (y + 2, 7, 6))):
            ref = half(origin, k, h if way == 0 else 1 - h)
            take(ref, two_recv.at[way, h])
            if h == 0:
                go(ref, half_send.at[way], half_recv.at[way], at_y(two))
            go(ref, three_send.at[way, h], three_recv.at[way], at_y(one))

    def gather_start():
        for h in range(2):
            go(half(y, k, h), two_send.at[0, h], two_recv.at[0, h], at_y(2))
            go(half(y, k, 1 - h), two_send.at[1, h], two_recv.at[1, h], at_y(6))
        go(mine, ring_send.at[1], ring_recv.at[1], at_y(1))
        go(mine, ring_send.at[7], ring_recv.at[7], at_y(7))
        go(mine, sib_send.at[0], sib_recv.at[0], sibling)

    def inverse_start():
        for i in (4, 3, 5, 2, 6, 1, 7):
            go(d_rows(y, k), d_send.at[i], d_recv.at[i], at_y(i))
        go(d_rows(y, k), dsib_send.at[0], dsib_recv.at[0], sibling)

    def gather_on():
        second_step(0)
        second_step(1)
        go(shard(y - 2, k), sib_send.at[2], sib_recv.at[2], sibling)
        go(shard(y + 2, k), sib_send.at[6], sib_recv.at[6], sibling)
        for i in (1, 7):
            take(shard(y - i, k), ring_recv.at[i])
            go(shard(y - i, k), sib_send.at[i], sib_recv.at[i], sibling)

    def inverse_on():
        for i in (1, 7, 2, 6, 3, 5, 4):
            hand_d(i)

    @pl.when(early)
    def _():
        inverse_start()
        gather_start()
        inverse_on()

    @pl.when(late_other)
    def _():
        for cc in range(2):
            pl.semaphore_signal(origin_ready, inc=1, device_id=(r, cc), device_id_type=MESH)

    @pl.when(late_origin)
    def _():
        pl.semaphore_wait(origin_ready, 14)

    @pl.when(late)
    def _():
        gather_start()
        gather_on()

    def hand_piece(b):
        piece = mir.at[b * 16 + slot]
        return remote(piece, piece, pass_send.at[b], pass_recv.at[b], (r + N_COL, c))

    def spread(b):
        piece = mir.at[b * 16 + slot]
        for n in HALF_PEERS:
            remote(piece, piece, mir_send, mir_recv.at[b], (r ^ n, c)).start()

    def solve(b):
        take(raw.at[b], raw_recv.at[b])
        solved = lax.dot_general(
            raw[b], dt[...], (((1,), (0,)), ((), ())), precision=HIGHEST, preferred_element_type=jnp.float32
        ).astype(jnp.bfloat16).astype(jnp.float32)
        mir[b * 16 + slot] = lax.dot_general(
            solved, dt[...], (((1,), (1,)), ((), ())), precision=HIGHEST, preferred_element_type=jnp.float32
        ).astype(jnp.bfloat16)

    def gather_end():
        for way, i in enumerate((3, 5)):
            take(shard(y - i, k), three_recv.at[way])
            go(shard(y - i, k), sib_send.at[i], sib_recv.at[i], sibling)
        take(half(y + 4, k, 0), half_recv.at[0])
        take(half(y + 4, k, 1), half_recv.at[1])
        go(shard(y + 4, k), sib_send.at[4], sib_recv.at[4], sibling)

    @pl.when(early)
    def _():
        for i in range(NY):
            take(d_rows(y - i, 1 - k), dsib_recv.at[i])
        solve(0)
        pl.semaphore_wait(ready, 1)
        hand_piece(0).start()
        spread(0)
        gather_on()
        solve(1)
        hand_piece(1).start()
        spread(1)
        gather_end()

    @pl.when(late)
    def _():
        gather_end()
        for b in range(2):
            take(mir.at[b * 16 + slot], pass_recv.at[b])
            spread(b)

    load_slab.wait()
    for i in (0, 2, 6, 1, 7, 3, 5, 4):
        take(shard(y - i, 1 - k), sib_recv.at[i])
    stores = []
    for b in range(2):
        take(mir.at[pl.ds(0, 15)], mir_recv.at[b])
        mirror = mir[b * 16:b * 16 + 16].reshape(NB, NB)
        cols = slice(b * NB, b * NB + NB)
        product = lax.dot_general(
            sol[...], mirror, (((1,), (1,)), ((), ())), preferred_element_type=jnp.float32
        )
        slab[:, cols] = (slab[:, cols].astype(jnp.float32) - product).astype(jnp.bfloat16)
        store = pltpu.make_async_copy(slab.at[:, cols], out.at[:, cols], out_sem.at[b])
        store.start()
        stores.append(store)

    for way in range(2):
        for h in range(2):
            take(sol.at[pl.ds(0, 64), :], two_send.at[way, h])
            take(sol.at[pl.ds(0, 64), :], three_send.at[way, h])
        take(sol.at[pl.ds(0, 64), :], half_send.at[way])
        take(sol.at[pl.ds(0, OWN), :], ring_send.at[1 + 6 * way])
    for i in range(NY):
        take(sol.at[pl.ds(0, OWN), :], sib_send.at[i])
    take(mir.at[pl.ds(0, 30)], mir_send)

    @pl.when(is_origin)
    def _():
        @pl.when(jnp.logical_not(own_origin))
        def _():
            direct(0).wait_send()

        for i in range(1, 8):
            direct(i).wait_send()

    @pl.when(early)
    def _():
        for i in range(NY):
            take(dt.at[pl.ds(0, 16), :], dsib_send.at[i])
            if i > 0:
                take(dt.at[pl.ds(0, 16), :], d_send.at[i])
        for b in range(2):
            hand_piece(b).wait_send()

    for store in stores:
        store.wait()


def local(trailing, panel, diag_inverse):
    dma = pltpu.SemaphoreType.DMA
    any_space = pl.BlockSpec(memory_space=pl.ANY)
    hbm = pl.BlockSpec(memory_space=pltpu.HBM)
    trailing, panel, dinv = (
        pltpu.with_memory_space_constraint(v, pltpu.HBM) for v in (trailing, panel, diag_inverse.T)
    )
    return pl.pallas_call(
        step_kernel,
        out_shape=jax.ShapeDtypeStruct(trailing.shape, trailing.dtype),
        in_specs=[hbm] * 3,
        out_specs=any_space,
        scratch_shapes=[
            pltpu.VMEM((2048, 512), jnp.bfloat16),
            pltpu.VMEM((128, 256), jnp.float32),
            pltpu.VMEM((256, 256), jnp.float32),
            pltpu.VMEM((2, 16, 256), jnp.float32),
            pltpu.VMEM((2048, 256), jnp.bfloat16),
            pltpu.VMEM((32, 16, 256), jnp.bfloat16),
            dma((3,)), dma((8,)), dma((8,)), dma((8,)), dma((8,)), dma((8,)), dma((2,)), dma((2,)), dma((2,)),
            pltpu.SemaphoreType.REGULAR(()), pltpu.SemaphoreType.REGULAR(()),
            dma((2, 2)), dma((2, 2)), dma((2,)), dma((2,)), dma((2, 2)), dma((2,)), dma((8,)), dma((8,)), dma((8,)), dma((8,)),
            dma(()), dma((2,)), dma((2,)),
        ],
        name="panel_step",
        compiler_params=pltpu.CompilerParams(
            collective_id=0, has_side_effects=True, vmem_limit_bytes=40 * 1024 * 1024
        ),
    )(trailing, panel, dinv)


def solution(mesh):
    in_specs = (P("row", "col"), P(("row", "col"), None), P(None, "col"))
    out_specs = P("row", "col")
    return jax.shard_map(local, mesh=mesh, in_specs=in_specs, out_specs=out_specs, check_vma=False)
```

```python
import jax
import jax.numpy as jnp
from jax import lax
from jax.experimental import pallas as pl
from jax.experimental.pallas import tpu as pltpu
from jax.sharding import PartitionSpec as P

MESH = pl.DeviceIdType.MESH
NB = 256
NY = 8
N_COL = 16
OWN = 128
PIECE = 16
HIGHEST = lax.Precision.HIGHEST


def remote(src, dst, send_sem, recv_sem, device):
    return pltpu.make_async_remote_copy(
        src_ref=src, dst_ref=dst, send_sem=send_sem, recv_sem=recv_sem,
        device_id=device, device_id_type=MESH,
    )


def take(ref, sem):
    pltpu.make_async_copy(ref, ref, sem).wait()


HALF_PEERS = (10, 14, 8, 9, 11, 12, 13, 15, 6, 2, 4, 5, 7, 1, 3)


def update(values, rows, pieces):
    product = lax.dot_general(
        rows, pieces.reshape(NB, NB), (((1,), (1,)), ((), ())), preferred_element_type=jnp.float32
    )
    return (values.astype(jnp.float32) - product).astype(jnp.bfloat16)


def last_block(slab, gathered, mirror, out, block, sem):
    left, right = pl.ds(0, NB), pl.ds(NB, NB)
    stores = []
    for n in range(4):
        span = pl.ds(n * 512, 512)
        stores.append(pltpu.make_async_copy(slab.at[span, left], out.at[span, left], sem.at[n]))
        stores[-1].start()
    for n in range(4):
        span = pl.ds(n * 512, 512)
        block[span, :] = update(slab[span, right], gathered[span, :], mirror[...])
        stores.append(pltpu.make_async_copy(block.at[span, :], out.at[span, right], sem.at[4 + n]))
        stores[-1].start()
    for store in stores:
        store.wait()


def step_kernel(
    trailing, panel, dinv, out, gathered, mirror,
    slab, rows, dt, raw, sol, mir,
    load_sem, d_send, d_recv, dsib_send, dsib_recv, raw_send, pass_send, pass_recv, raw_recv,
    ready, origin_ready, two_send, two_recv, half_send, half_recv, three_send, three_recv, ring_send, ring_recv, sib_send, sib_recv,
    mir_send, mir_recv, out_sem,
):
    r, c = lax.axis_index("row"), lax.axis_index("col")
    y, k = c >> 1, c & 1
    sibling = (r, c ^ 1)
    block = r >> 4
    slot = r & 15
    early = block == 0
    late = block == 1
    is_origin = c < 2
    own_origin = jnp.logical_and(r == 0, c == 0)

    def at_y(step):
        return (r, (c + 2 * step) & 15)

    def d_rows(yy, kk):
        return dt.at[pl.ds(pl.multiple_of((yy & 7) * 32 + kk * 16, 16), 16), :]

    load_panel = pltpu.make_async_copy(panel, rows, load_sem.at[0])
    load_dinv = pltpu.make_async_copy(dinv, d_rows(y, k), load_sem.at[1])
    load_slab = pltpu.make_async_copy(trailing, slab, load_sem.at[2])
    load_panel.start()
    load_dinv.start()
    load_slab.start()

    barrier = pltpu.get_barrier_semaphore()

    def greet(device):
        pl.semaphore_signal(barrier, inc=1, device_id=device, device_id_type=MESH)

    @pl.when(early)
    def _():
        greet((c + N_COL, r >> 3))
        greet((r + N_COL, c))

        @pl.when(jnp.logical_not(own_origin))
        def _():
            greet((c, r >> 3))

    late_origin = jnp.logical_and(late, is_origin)
    other = jnp.logical_not(is_origin)
    for n in range(1, N_COL):
        @pl.when(jnp.logical_not(jnp.logical_and(other, (c ^ n) < 2)))
        def _():
            greet((r, c ^ n))

    for n in HALF_PEERS:
        greet((r ^ n, c))

    def shard(yy, kk):
        return sol.at[pl.ds(pl.multiple_of((yy & 7) * 256 + kk * OWN, OWN), OWN), :]

    def half(yy, kk, j):
        return sol.at[pl.ds(pl.multiple_of((yy & 7) * 256 + kk * OWN + j * 64, 64), 64), :]

    mine = shard(y, k)
    load_panel.wait()
    mine[...] = rows[...].astype(jnp.bfloat16)
    load_dinv.wait()
    pl.semaphore_wait(barrier, 30 + block + jnp.where(is_origin, 8, 0) - jnp.where(own_origin, 1, 0) - jnp.where(is_origin, 14, 0))

    def direct(i):
        src = rows.at[pl.ds(i * PIECE, PIECE), :]
        return remote(src, raw.at[block], raw_send.at[i], raw_recv.at[block], (8 * k + i, slot))

    @pl.when(is_origin)
    def _():
        @pl.when(jnp.logical_not(own_origin))
        def _():
            direct(0).start()

        @pl.when(own_origin)
        def _():
            pltpu.make_async_copy(rows.at[pl.ds(0, PIECE), :], raw.at[0], raw_recv.at[0]).start()

        for i in range(1, 8):
            direct(i).start()

    @pl.when(late)
    def _():
        pl.semaphore_signal(ready, inc=1, device_id=(r - N_COL, c), device_id_type=MESH)

    def go(src, send_sem, recv_sem, device):
        copy = remote(src, src, send_sem, recv_sem, device)
        copy.start()

    def hand_d(i):
        ref = d_rows(y - i, k)
        take(ref, d_recv.at[i])
        copy = remote(ref, ref, dsib_send.at[i], dsib_recv.at[i], sibling)
        copy.start()

    def second_step(h):
        for way, (origin, one, two) in enumerate(((y - 2, 1, 2), (y + 2, 7, 6))):
            ref = half(origin, k, h if way == 0 else 1 - h)
            take(ref, two_recv.at[way, h])
            if h == 0:
                go(ref, half_send.at[way], half_recv.at[way], at_y(two))
            go(ref, three_send.at[way, h], three_recv.at[way], at_y(one))

    def gather_start():
        for h in range(2):
            go(half(y, k, h), two_send.at[0, h], two_recv.at[0, h], at_y(2))
            go(half(y, k, 1 - h), two_send.at[1, h], two_recv.at[1, h], at_y(6))
        go(mine, ring_send.at[1], ring_recv.at[1], at_y(1))
        go(mine, ring_send.at[7], ring_recv.at[7], at_y(7))
        go(mine, sib_send.at[0], sib_recv.at[0], sibling)

    def inverse_start():
        for i in (4, 3, 5, 2, 6, 1, 7):
            go(d_rows(y, k), d_send.at[i], d_recv.at[i], at_y(i))
        go(d_rows(y, k), dsib_send.at[0], dsib_recv.at[0], sibling)

    def gather_on():
        second_step(0)
        second_step(1)
        go(shard(y - 2, k), sib_send.at[2], sib_recv.at[2], sibling)
        go(shard(y + 2, k), sib_send.at[6], sib_recv.at[6], sibling)
        for i in (1, 7):
            take(shard(y - i, k), ring_recv.at[i])
            go(shard(y - i, k), sib_send.at[i], sib_recv.at[i], sibling)

    def inverse_on():
        for i in (1, 7, 2, 6, 3, 5, 4):
            hand_d(i)

    @pl.when(other)
    def _():
        for cc in range(2):
            pl.semaphore_signal(origin_ready, inc=1, device_id=(r, cc), device_id_type=MESH)

    @pl.when(is_origin)
    def _():
        pl.semaphore_wait(origin_ready, 14)

    @pl.when(early)
    def _():
        inverse_start()
        gather_start()
        inverse_on()

    @pl.when(late)
    def _():
        gather_start()
        gather_on()

    def hand_piece(b):
        piece = mir.at[b * 16 + slot]
        return remote(piece, piece, pass_send.at[b], pass_recv.at[b], (r + N_COL, c))

    def spread(b):
        piece = mir.at[b * 16 + slot]
        for n in HALF_PEERS:
            remote(piece, piece, mir_send, mir_recv.at[b], (r ^ n, c)).start()

    def solve(b):
        take(raw.at[b], raw_recv.at[b])
        solved = lax.dot_general(
            raw[b], dt[...], (((1,), (0,)), ((), ())), precision=HIGHEST, preferred_element_type=jnp.float32
        ).astype(jnp.bfloat16).astype(jnp.float32)
        mir[b * 16 + slot] = lax.dot_general(
            solved, dt[...], (((1,), (1,)), ((), ())), precision=HIGHEST, preferred_element_type=jnp.float32
        ).astype(jnp.bfloat16)

    def gather_end():
        for way, i in enumerate((3, 5)):
            take(shard(y - i, k), three_recv.at[way])
            go(shard(y - i, k), sib_send.at[i], sib_recv.at[i], sibling)
        take(half(y + 4, k, 0), half_recv.at[0])
        take(half(y + 4, k, 1), half_recv.at[1])
        go(shard(y + 4, k), sib_send.at[4], sib_recv.at[4], sibling)

    @pl.when(early)
    def _():
        for i in range(NY):
            take(d_rows(y - i, 1 - k), dsib_recv.at[i])
        solve(0)
        pl.semaphore_wait(ready, 1)
        hand_piece(0).start()
        spread(0)
        gather_on()
        solve(1)
        hand_piece(1).start()
        spread(1)
        gather_end()

    @pl.when(late)
    def _():
        gather_end()
        for b in range(2):
            take(mir.at[b * 16 + slot], pass_recv.at[b])
            spread(b)

    load_slab.wait()
    left, right = pl.ds(0, NB), pl.ds(NB, NB)
    stores = [pltpu.make_async_copy(slab.at[:, right], out.at[:, right], out_sem.at[0])]
    stores[0].start()
    for i in (0, 2, 6, 1, 7, 3, 5, 4):
        take(shard(y - i, 1 - k), sib_recv.at[i])
    stores.append(pltpu.make_async_copy(sol, gathered, out_sem.at[1]))
    stores[1].start()
    take(mir.at[pl.ds(0, 15)], mir_recv.at[0])
    slab[:, left] = update(slab[:, left], sol[...], mir[:16])
    stores.append(pltpu.make_async_copy(slab.at[:, left], out.at[:, left], out_sem.at[2]))
    stores[2].start()
    take(mir.at[pl.ds(0, 15)], mir_recv.at[1])
    stores.append(pltpu.make_async_copy(mir.at[pl.ds(16, 16)], mirror, out_sem.at[3]))
    stores[3].start()

    for way in range(2):
        for h in range(2):
            take(sol.at[pl.ds(0, 64), :], two_send.at[way, h])
            take(sol.at[pl.ds(0, 64), :], three_send.at[way, h])
        take(sol.at[pl.ds(0, 64), :], half_send.at[way])
        take(sol.at[pl.ds(0, OWN), :], ring_send.at[1 + 6 * way])
    for i in range(NY):
        take(sol.at[pl.ds(0, OWN), :], sib_send.at[i])
    take(mir.at[pl.ds(0, 30)], mir_send)

    @pl.when(is_origin)
    def _():
        @pl.when(jnp.logical_not(own_origin))
        def _():
            direct(0).wait_send()

        for i in range(1, 8):
            direct(i).wait_send()

    @pl.when(early)
    def _():
        for i in range(NY):
            take(dt.at[pl.ds(0, 16), :], dsib_send.at[i])
            if i > 0:
                take(dt.at[pl.ds(0, 16), :], d_send.at[i])
        for b in range(2):
            hand_piece(b).wait_send()

    for store in stores:
        store.wait()


def local(trailing, panel, diag_inverse):
    dma = pltpu.SemaphoreType.DMA
    any_space = pl.BlockSpec(memory_space=pl.ANY)
    hbm = pl.BlockSpec(memory_space=pltpu.HBM)
    trailing, panel, dinv = (
        pltpu.with_memory_space_constraint(v, pltpu.HBM) for v in (trailing, panel, diag_inverse.T)
    )
    parts = pl.pallas_call(
        step_kernel,
        out_shape=[
            jax.ShapeDtypeStruct((2048, 512), jnp.bfloat16),
            jax.ShapeDtypeStruct((2048, 256), jnp.bfloat16),
            jax.ShapeDtypeStruct((16, 16, 256), jnp.bfloat16),
        ],
        in_specs=[hbm] * 3,
        out_specs=[any_space] * 3,
        scratch_shapes=[
            pltpu.VMEM((2048, 512), jnp.bfloat16),
            pltpu.VMEM((128, 256), jnp.float32),
            pltpu.VMEM((256, 256), jnp.float32),
            pltpu.VMEM((2, 16, 256), jnp.float32),
            pltpu.VMEM((2048, 256), jnp.bfloat16),
            pltpu.VMEM((32, 16, 256), jnp.bfloat16),
            dma((3,)), dma((8,)), dma((8,)), dma((8,)), dma((8,)), dma((8,)), dma((2,)), dma((2,)), dma((2,)),
            pltpu.SemaphoreType.REGULAR(()), pltpu.SemaphoreType.REGULAR(()),
            dma((2, 2)), dma((2, 2)), dma((2,)), dma((2,)), dma((2, 2)), dma((2,)), dma((8,)), dma((8,)), dma((8,)), dma((8,)),
            dma(()), dma((2,)), dma((4,)),
        ],
        name="panel_step",
        compiler_params=pltpu.CompilerParams(
            collective_id=0, has_side_effects=True, vmem_limit_bytes=40 * 1024 * 1024
        ),
    )(trailing, panel, dinv)
    return pl.pallas_call(
        last_block,
        out_shape=jax.ShapeDtypeStruct((2048, 512), jnp.bfloat16),
        in_specs=[pl.BlockSpec(memory_space=pltpu.VMEM)] * 3,
        out_specs=hbm,
        scratch_shapes=[pltpu.VMEM((2048, 256), jnp.bfloat16), dma((8,))],
        name="last_block",
        compiler_params=pltpu.CompilerParams(vmem_limit_bytes=24 * 1024 * 1024),
    )(*(pltpu.with_memory_space_constraint(v, pltpu.VMEM) for v in parts))


def solution(mesh):
    in_specs = (P("row", "col"), P(("row", "col"), None), P(None, "col"))
    out_specs = P("row", "col")
    return jax.shard_map(local, mesh=mesh, in_specs=in_specs, out_specs=out_specs, check_vma=False)
```

```python
import jax
import jax.numpy as jnp
from jax import lax
from jax.experimental import pallas as pl
from jax.experimental.pallas import tpu as pltpu
from jax.sharding import PartitionSpec as P

MESH = pl.DeviceIdType.MESH
NB = 256
NY = 8
N_COL = 16
OWN = 128
PIECE = 16
HIGHEST = lax.Precision.HIGHEST


def remote(src, dst, send_sem, recv_sem, device):
    return pltpu.make_async_remote_copy(
        src_ref=src, dst_ref=dst, send_sem=send_sem, recv_sem=recv_sem,
        device_id=device, device_id_type=MESH,
    )


def take(ref, sem):
    pltpu.make_async_copy(ref, ref, sem).wait()


HALF_PEERS = (10, 14, 8, 9, 11, 12, 13, 15, 6, 2, 4, 5, 7, 1, 3)


def update(values, rows, pieces):
    product = lax.dot_general(
        rows, pieces.reshape(NB, NB), (((1,), (1,)), ((), ())), preferred_element_type=jnp.float32
    )
    return (values.astype(jnp.float32) - product).astype(jnp.bfloat16)


def last_block(slab, gathered, mirror, out, block, sem):
    left, right = pl.ds(0, NB), pl.ds(NB, NB)
    stores = []
    for n in range(4):
        span = pl.ds(n * 512, 512)
        stores.append(pltpu.make_async_copy(slab.at[span, left], out.at[span, left], sem.at[n]))
        stores[-1].start()
    for n in range(4):
        span = pl.ds(n * 512, 512)
        block[span, :] = update(slab[span, right], gathered[span, :], mirror[...])
        stores.append(pltpu.make_async_copy(block.at[span, :], out.at[span, right], sem.at[4 + n]))
        stores[-1].start()
    for store in stores:
        store.wait()


def step_kernel(
    trailing, panel, dinv, out, gathered, mirror,
    slab, rows, dt, dt_high, dt_low, raw, sol, mir,
    load_sem, d_send, d_recv, dsib_send, dsib_recv, raw_send, pass_send, pass_recv, raw_recv,
    ready, origin_ready, two_send, two_recv, half_send, half_recv, three_send, three_recv, ring_send, ring_recv, sib_send, sib_recv,
    mir_send, mir_recv, out_sem,
):
    r, c = lax.axis_index("row"), lax.axis_index("col")
    y, k = c >> 1, c & 1
    sibling = (r, c ^ 1)
    block = r >> 4
    slot = r & 15
    early = block == 0
    late = block == 1
    is_origin = c < 2
    own_origin = jnp.logical_and(r == 0, c == 0)

    def at_y(step):
        return (r, (c + 2 * step) & 15)

    def d_rows(yy, kk):
        return dt.at[pl.ds(pl.multiple_of((yy & 7) * 32 + kk * 16, 16), 16), :]

    load_panel = pltpu.make_async_copy(panel, rows, load_sem.at[0])
    load_dinv = pltpu.make_async_copy(dinv, d_rows(y, k), load_sem.at[1])
    load_slab = pltpu.make_async_copy(trailing, slab, load_sem.at[2])
    load_panel.start()
    load_dinv.start()
    load_slab.start()

    barrier = pltpu.get_barrier_semaphore()

    def greet(device):
        pl.semaphore_signal(barrier, inc=1, device_id=device, device_id_type=MESH)

    @pl.when(early)
    def _():
        greet((c + N_COL, r >> 3))
        greet((r + N_COL, c))

        @pl.when(jnp.logical_not(own_origin))
        def _():
            greet((c, r >> 3))

    late_origin = jnp.logical_and(late, is_origin)
    other = jnp.logical_not(is_origin)
    for n in HALF_PEERS:
        greet((r ^ n, c))

    for n in range(1, N_COL):
        @pl.when(jnp.logical_not(jnp.logical_and(other, (c ^ n) < 2)))
        def _():
            greet((r, c ^ n))

    def shard(yy, kk):
        return sol.at[pl.ds(pl.multiple_of((yy & 7) * 256 + kk * OWN, OWN), OWN), :]

    def half(yy, kk, j):
        return sol.at[pl.ds(pl.multiple_of((yy & 7) * 256 + kk * OWN + j * 64, 64), 64), :]

    mine = shard(y, k)
    load_panel.wait()
    mine[...] = rows[...].astype(jnp.bfloat16)
    load_dinv.wait()
    pl.semaphore_wait(barrier, 30 + block + jnp.where(is_origin, 8, 0) - jnp.where(own_origin, 1, 0) - jnp.where(is_origin, 14, 0))

    def direct(i):
        src = rows.at[pl.ds(i * PIECE, PIECE), :]
        return remote(src, raw.at[block], raw_send.at[i], raw_recv.at[block], (8 * k + i, slot))

    @pl.when(is_origin)
    def _():
        @pl.when(jnp.logical_not(own_origin))
        def _():
            direct(0).start()

        @pl.when(own_origin)
        def _():
            pltpu.make_async_copy(rows.at[pl.ds(0, PIECE), :], raw.at[0], raw_recv.at[0]).start()

        for i in range(1, 8):
            direct(i).start()

    @pl.when(late)
    def _():
        pl.semaphore_signal(ready, inc=1, device_id=(r - N_COL, c), device_id_type=MESH)

    def go(src, send_sem, recv_sem, device):
        copy = remote(src, src, send_sem, recv_sem, device)
        copy.start()

    def hand_d(i):
        ref = d_rows(y - i, k)
        take(ref, d_recv.at[i])
        copy = remote(ref, ref, dsib_send.at[i], dsib_recv.at[i], sibling)
        copy.start()

    def second_step(h):
        for way, (origin, one, two) in enumerate(((y - 2, 1, 2), (y + 2, 7, 6))):
            ref = half(origin, k, h if way == 0 else 1 - h)
            take(ref, two_recv.at[way, h])
            if h == 0:
                go(ref, half_send.at[way], half_recv.at[way], at_y(two))
            go(ref, three_send.at[way, h], three_recv.at[way], at_y(one))

    def gather_start():
        for h in range(2):
            go(half(y, k, h), two_send.at[0, h], two_recv.at[0, h], at_y(2))
            go(half(y, k, 1 - h), two_send.at[1, h], two_recv.at[1, h], at_y(6))
        go(mine, ring_send.at[1], ring_recv.at[1], at_y(1))
        go(mine, ring_send.at[7], ring_recv.at[7], at_y(7))
        go(mine, sib_send.at[0], sib_recv.at[0], sibling)

    def inverse_start():
        for i in (4, 3, 5, 2, 6, 1, 7):
            go(d_rows(y, k), d_send.at[i], d_recv.at[i], at_y(i))
        go(d_rows(y, k), dsib_send.at[0], dsib_recv.at[0], sibling)

    def gather_on():
        second_step(0)
        second_step(1)
        go(shard(y - 2, k), sib_send.at[2], sib_recv.at[2], sibling)
        go(shard(y + 2, k), sib_send.at[6], sib_recv.at[6], sibling)
        for i in (1, 7):
            take(shard(y - i, k), ring_recv.at[i])
            go(shard(y - i, k), sib_send.at[i], sib_recv.at[i], sibling)

    def inverse_on():
        for i in (1, 7, 2, 6, 3, 5, 4):
            hand_d(i)

    @pl.when(other)
    def _():
        for cc in range(2):
            pl.semaphore_signal(origin_ready, inc=1, device_id=(r, cc), device_id_type=MESH)

    @pl.when(is_origin)
    def _():
        pl.semaphore_wait(origin_ready, 14)

    @pl.when(early)
    def _():
        inverse_start()
        gather_start()
        inverse_on()

    @pl.when(late)
    def _():
        gather_start()
        gather_on()

    def hand_piece(b):
        piece = mir.at[b * 16 + slot]
        return remote(piece, piece, pass_send.at[b], pass_recv.at[b], (r + N_COL, c))

    def spread(b):
        piece = mir.at[b * 16 + slot]
        for n in HALF_PEERS:
            remote(piece, piece, mir_send, mir_recv.at[b], (r ^ n, c)).start()

    def solve(b):
        take(raw.at[b], raw_recv.at[b])
        solved = lax.dot_general(
            raw[b], dt[...], (((1,), (0,)), ((), ())), precision=HIGHEST, preferred_element_type=jnp.float32
        ).astype(jnp.bfloat16)
        high, low = (
            lax.dot_general(solved, part[...], (((1,), (1,)), ((), ())), preferred_element_type=jnp.float32)
            for part in (dt_high, dt_low)
        )
        mir[b * 16 + slot] = (high + low).astype(jnp.bfloat16)

    def gather_end():
        for way, i in enumerate((3, 5)):
            take(shard(y - i, k), three_recv.at[way])
            go(shard(y - i, k), sib_send.at[i], sib_recv.at[i], sibling)
        take(half(y + 4, k, 0), half_recv.at[0])
        take(half(y + 4, k, 1), half_recv.at[1])
        go(shard(y + 4, k), sib_send.at[4], sib_recv.at[4], sibling)

    @pl.when(early)
    def _():
        for i in range(NY):
            take(d_rows(y - i, 1 - k), dsib_recv.at[i])
        dt_high[...] = dt[...].astype(jnp.bfloat16)
        dt_low[...] = (dt[...] - dt_high[...].astype(jnp.float32)).astype(jnp.bfloat16)
        solve(0)
        pl.semaphore_wait(ready, 1)
        hand_piece(0).start()
        spread(0)
        gather_on()
        solve(1)
        hand_piece(1).start()
        spread(1)
        gather_end()

    @pl.when(late)
    def _():
        gather_end()
        for b in range(2):
            take(mir.at[b * 16 + slot], pass_recv.at[b])
            spread(b)

    load_slab.wait()
    left, right = pl.ds(0, NB), pl.ds(NB, NB)
    stores = [pltpu.make_async_copy(slab.at[:, right], out.at[:, right], out_sem.at[0])]
    stores[0].start()
    for i in (0, 2, 6, 1, 7, 3, 5, 4):
        take(shard(y - i, 1 - k), sib_recv.at[i])
    stores.append(pltpu.make_async_copy(sol, gathered, out_sem.at[1]))
    stores[1].start()
    take(mir.at[pl.ds(0, 15)], mir_recv.at[0])
    slab[:, left] = update(slab[:, left], sol[...], mir[:16])
    stores.append(pltpu.make_async_copy(slab.at[:, left], out.at[:, left], out_sem.at[2]))
    stores[2].start()
    take(mir.at[pl.ds(0, 15)], mir_recv.at[1])
    stores.append(pltpu.make_async_copy(mir.at[pl.ds(16, 16)], mirror, out_sem.at[3]))
    stores[3].start()

    for way in range(2):
        for h in range(2):
            take(sol.at[pl.ds(0, 64), :], two_send.at[way, h])
            take(sol.at[pl.ds(0, 64), :], three_send.at[way, h])
        take(sol.at[pl.ds(0, 64), :], half_send.at[way])
        take(sol.at[pl.ds(0, OWN), :], ring_send.at[1 + 6 * way])
    for i in range(NY):
        take(sol.at[pl.ds(0, OWN), :], sib_send.at[i])
    take(mir.at[pl.ds(0, 30)], mir_send)

    @pl.when(is_origin)
    def _():
        @pl.when(jnp.logical_not(own_origin))
        def _():
            direct(0).wait_send()

        for i in range(1, 8):
            direct(i).wait_send()

    @pl.when(early)
    def _():
        for i in range(NY):
            take(dt.at[pl.ds(0, 16), :], dsib_send.at[i])
            if i > 0:
                take(dt.at[pl.ds(0, 16), :], d_send.at[i])
        for b in range(2):
            hand_piece(b).wait_send()

    for store in stores:
        store.wait()


def local(trailing, panel, diag_inverse):
    dma = pltpu.SemaphoreType.DMA
    any_space = pl.BlockSpec(memory_space=pl.ANY)
    hbm = pl.BlockSpec(memory_space=pltpu.HBM)
    trailing, panel, dinv = (
        pltpu.with_memory_space_constraint(v, pltpu.HBM) for v in (trailing, panel, diag_inverse.T)
    )
    parts = pl.pallas_call(
        step_kernel,
        out_shape=[
            jax.ShapeDtypeStruct((2048, 512), jnp.bfloat16),
            jax.ShapeDtypeStruct((2048, 256), jnp.bfloat16),
            jax.ShapeDtypeStruct((16, 16, 256), jnp.bfloat16),
        ],
        in_specs=[hbm] * 3,
        out_specs=[any_space] * 3,
        scratch_shapes=[
            pltpu.VMEM((2048, 512), jnp.bfloat16),
            pltpu.VMEM((128, 256), jnp.float32),
            pltpu.VMEM((256, 256), jnp.float32),
            pltpu.VMEM((256, 256), jnp.bfloat16),
            pltpu.VMEM((256, 256), jnp.bfloat16),
            pltpu.VMEM((2, 16, 256), jnp.float32),
            pltpu.VMEM((2048, 256), jnp.bfloat16),
            pltpu.VMEM((32, 16, 256), jnp.bfloat16),
            dma((3,)), dma((8,)), dma((8,)), dma((8,)), dma((8,)), dma((8,)), dma((2,)), dma((2,)), dma((2,)),
            pltpu.SemaphoreType.REGULAR(()), pltpu.SemaphoreType.REGULAR(()),
            dma((2, 2)), dma((2, 2)), dma((2,)), dma((2,)), dma((2, 2)), dma((2,)), dma((8,)), dma((8,)), dma((8,)), dma((8,)),
            dma(()), dma((2,)), dma((4,)),
        ],
        name="panel_step",
        compiler_params=pltpu.CompilerParams(
            collective_id=0, has_side_effects=True, vmem_limit_bytes=40 * 1024 * 1024
        ),
    )(trailing, panel, dinv)
    return pl.pallas_call(
        last_block,
        out_shape=jax.ShapeDtypeStruct((2048, 512), jnp.bfloat16),
        in_specs=[pl.BlockSpec(memory_space=pltpu.VMEM)] * 3,
        out_specs=hbm,
        scratch_shapes=[pltpu.VMEM((2048, 256), jnp.bfloat16), dma((8,))],
        name="last_block",
        compiler_params=pltpu.CompilerParams(vmem_limit_bytes=24 * 1024 * 1024),
    )(*(pltpu.with_memory_space_constraint(v, pltpu.VMEM) for v in parts))


def solution(mesh):
    in_specs = (P("row", "col"), P(("row", "col"), None), P(None, "col"))
    out_specs = P("row", "col")
    return jax.shard_map(local, mesh=mesh, in_specs=in_specs, out_specs=out_specs, check_vma=False)
```
